32 devices in a mesh: scen: 4 (over z), slab: 2 (over x), grp: 4 (over y, core).
Axes of the slice: x: 2, y: 2, z: 4, core: 2. Of those that a mesh axis runs over, the one named last changes fastest.
Arguments:
- factor_inverse: bfloat16 [4, 1536, 1536], P('grp', ('scen', 'slab')), may hold values from -0.102062073 to 2, as said below
- border_window: bfloat16 [4, 1536, 2048], P('grp', None, ('scen', 'slab')), may hold values from -0.47851562 to 0.47851562
- border_panel: bfloat16 [4, 1536, 1024], P('grp', None, 'slab'), may hold values from -0.47851562 to 0.47851562
- border_pattern: int32 [4, 16], P('grp', ('scen', 'slab')), may hold values 0 or 1
- earlier_rows: bfloat16 [4096, 2048], P('grp', ('scen', 'slab')), may hold values from -0.75 to 0.75
- earlier_panel: bfloat16 [4096, 1024], P('grp'), may hold values from -0.75 to 0.75
- pivot_inverse: bfloat16 [1024, 1024], P('grp'), may hold values from -0.125 to 2, as said below
Outputs:
- panel_factor: bfloat16 [1024, 2048], P('grp', ('scen', 'slab'))
The draws below stay inside these ranges and needn't reach their ends.
Inputs may be any that keep to these rules, and one draw needn't show every extreme that they name: factor_inverse[s, k, i] is zero where i < k; its diagonal lies between 0.5 and 2. pivot_inverse[j, k] is zero where k > j; its diagonal lies between 0.5 and 2.
All inputs are finite; a program needn't handle non-finite values. No bound on the sum of `border_pattern` on one device may be relied on, other than what follows from the above.
Results may differ from the reference program's by a relative error of at most 0.0056.
Values may be sent and summed in bfloat16 or wider, within the bound.
A program may use at most 64 MiB of HBM per device.

```python
import math
import jax
import jax.numpy as jnp
from jax import lax

K = 1536
C = 1024
E = 4096
BLK = 128
SCENARIOS = 4
ROWS = 2048


def draw_factor_inverse(key, part):
    first, second = jax.random.split(jax.random.fold_in(key, 11))
    spread = jnp.clip(jax.random.normal(first, (SCENARIOS, K, K), jnp.float32), -4.0, 4.0)
    diagonal = jnp.exp(jax.random.uniform(second, (SCENARIOS, K), jnp.float32, math.log(0.5), math.log(2.0)))
    upper = jnp.triu(spread, 1) / math.sqrt(K)
    identity = jnp.eye(K, dtype=jnp.float32)
    return (upper + identity[None, :, :] * diagonal[:, :, None]).astype(jnp.bfloat16)


def draw_pivot_inverse(key, part):
    first, second = jax.random.split(jax.random.fold_in(key, 23))
    spread = jnp.clip(jax.random.normal(first, (C, C), jnp.float32), -4.0, 4.0)
    diagonal = jnp.exp(jax.random.uniform(second, (C,), jnp.float32, math.log(0.5), math.log(2.0)))
    lower = jnp.tril(spread, -1) / math.sqrt(C)
    identity = jnp.eye(C, dtype=jnp.float32)
    return (lower + identity * diagonal[:, None]).astype(jnp.bfloat16)


def set_ends(array, own_key, smallest, top_value):
    longest = array.shape.index(max(array.shape))
    spots = []
    for shift in (0, 1):
        where = [jax.random.randint(jax.random.fold_in(own_key, axis), (), 0, length) for axis, length in enumerate(array.shape)]
        where[longest] = (where[longest] + shift) % array.shape[longest]
        spots.append(tuple(where))
    return array.at[spots[0]].set(smallest).at[spots[1]].set(top_value)


def levels(stream_key, extent, cuts, low, largest):
    def one(position, blocks):
        heights = jax.random.uniform(jax.random.fold_in(jax.random.fold_in(stream_key, 6), position), (blocks,), jnp.float32, low / len(cuts), largest / len(cuts))
        return jnp.repeat(jnp.exp(heights), extent[position] // blocks).reshape((-1,) + (1,) * (len(extent) - position - 1))

    loudness = one(*cuts[0])
    for cut in cuts[1:]:
        loudness = loudness * one(*cut)
    return loudness


def normal_values(rng, extent, width, bound, cuts=(), kind=jnp.bfloat16):
    values = width * jax.random.normal(rng, extent, jnp.float32)
    if cuts:
        values = values * levels(rng, extent, cuts, -0.22, 0.18)
    return jnp.clip(values, -bound, bound).astype(kind)


def setup_inputs(seed: int = 0) -> dict:
    keys = jax.random.split(jax.random.key(seed), 8)
    return {
        "factor_inverse": draw_factor_inverse(jax.random.fold_in(keys[7], 71), 0),
        "border_window": normal_values(keys[1], (SCENARIOS, K, ROWS), (0.5 * K ** -0.25), 0.47851562, ((0, 4), (2, 8))),
        "border_panel": normal_values(keys[2], (SCENARIOS, K, C), (0.5 * K ** -0.25), 0.47851562, ((0, 4), (2, 2))),
        "border_pattern": set_ends((jax.random.randint(keys[3], (SCENARIOS, ROWS // BLK), 0, 4) < 3).astype(jnp.int32), jax.random.fold_in(keys[3], 1), 0, 1),
        "earlier_rows": normal_values(keys[4], (E, ROWS), (E ** -0.25), 0.75, ((0, 4), (1, 8))),
        "earlier_panel": normal_values(keys[5], (E, C), (E ** -0.25), 0.75, ((0, 4),)),
        "pivot_inverse": draw_pivot_inverse(jax.random.fold_in(keys[7], 71), 0),
    }


def reference(factor_inverse, border_window, border_panel, border_pattern, earlier_rows, earlier_panel, pivot_inverse):
    column_mask = jnp.repeat(border_pattern.astype(jnp.bfloat16), BLK, axis=1)

    def scenario(summed, inputs):
        inverse_stored, window, blocks_mask, panel_border = inputs
        masked = window * blocks_mask[None, :]
        window_image = jnp.dot(inverse_stored.T, masked, preferred_element_type=jnp.float32).astype(jnp.bfloat16)
        panel_image = jnp.dot(inverse_stored.T, panel_border, preferred_element_type=jnp.float32).astype(jnp.bfloat16)
        return summed + jnp.dot(panel_image.T, window_image, preferred_element_type=jnp.float32), None

    initial = jnp.zeros((C, ROWS), jnp.float32)
    summed, unused = lax.scan(scenario, initial, (factor_inverse, border_window, column_mask, border_panel))
    update = jnp.dot(earlier_panel.T, earlier_rows, preferred_element_type=jnp.float32)
    schur_block = (summed - update).astype(jnp.bfloat16)
    return jnp.dot(pivot_inverse, schur_block, preferred_element_type=jnp.float32).astype(jnp.bfloat16)
```

```python
import functools

import jax
import jax.numpy as jnp
from jax import lax
from jax.experimental import pallas as pl
from jax.experimental.pallas import tpu as pltpu
from jax.sharding import PartitionSpec as P


F32 = jnp.float32
BF16 = jnp.bfloat16
MESH = pl.DeviceIdType.MESH


def event_codes(nz):
    codes = []
    for z in range(nz):
        pairs = sorted(range(nz), key=lambda p: (abs(p - z), p < z))
        events = [(p, j) for p in pairs for j in range(p, nz)]
        codes.append(
            (
                sum(p * nz**e for e, (p, j) in enumerate(events)),
                sum(j * nz**e for e, (p, j) in enumerate(events)),
            )
        )
    return codes


def pick(index, values):
    chosen = jnp.int32(values[0])
    for i, value in enumerate(values[1:], 1):
        chosen = jnp.where(index == i, jnp.int32(value), chosen)
    return chosen


def panel_kernel(
    nz,
    f_in,
    bw_in,
    bp_in,
    pat,
    er_in,
    ep_in,
    pv_in,
    out,
    fg,
    bw,
    bp,
    er,
    ep,
    pv,
    bt,
    acc,
    tot,
    half,
    ybuf,
    yrecv,
    sch,
    loc_sem,
    f_recv,
    up_sem,
    dn_sem,
    xs_sem,
    bp_send,
    bp_recv,
    c_send,
    c_recv,
    y_send,
    y_recv,
    s_send,
    s_fwd,
    s_recv,
):
    z = lax.axis_index("scen")
    x = lax.axis_index("slab")
    g = lax.axis_index("grp")
    ox = 1 - x
    core = g + 1 - 2 * lax.rem(g, 2)
    far = lax.rem(g + 2, 4)
    last = nz - 1
    rows = f_in.shape[1]
    order = f_in.shape[2]
    wide = order // nz
    pc = bp_in.shape[2]
    wc = bw_in.shape[2]
    count = nz * (nz + 1) // 2
    codes = event_codes(nz)
    code_p = pick(z, [c[0] for c in codes])
    code_j = pick(z, [c[1] for c in codes])
    up_id, dn_id, x_id = {"scen": z + 1}, {"scen": z - 1}, {"slab": ox}

    own = 2 * z + x
    locals_ = [
        pltpu.make_async_copy(f_in.at[0], fg.at[own], loc_sem.at[0]),
        pltpu.make_async_copy(bw_in.at[0], bw, loc_sem.at[1]),
        pltpu.make_async_copy(bp_in.at[0], bp.at[x], loc_sem.at[2]),
        pltpu.make_async_copy(er_in, er, loc_sem.at[3]),
        pltpu.make_async_copy(ep_in, ep, loc_sem.at[4]),
        pltpu.make_async_copy(pv_in, pv, loc_sem.at[5]),
    ]
    for c in locals_:
        c.start()

    barrier = pltpu.get_barrier_semaphore()

    @pl.when(z < last)
    def _():
        pl.semaphore_signal(barrier, inc=1, device_id=up_id, device_id_type=MESH)

    @pl.when(z > 0)
    def _():
        pl.semaphore_signal(barrier, inc=1, device_id=dn_id, device_id_type=MESH)

    for peer in (x_id, {"grp": core}, {"grp": far}):
        pl.semaphore_signal(barrier, inc=1, device_id=peer, device_id_type=MESH)
    pl.semaphore_wait(barrier, 3 + jnp.where(z < last, 1, 0) + jnp.where(z > 0, 1, 0))

    def cols(j):
        return pl.ds(pl.multiple_of(j * wide, 128), wide)

    def piece(d, j, sems, peer, src=None):
        here = fg.at[d, :, cols(j)]
        return pltpu.make_async_remote_copy(
            src_ref=here if src is None else src,
            dst_ref=here,
            send_sem=sems.at[d, j],
            recv_sem=f_recv.at[d, j],
            device_id=peer,
            device_id_type=MESH,
        )

    def goes_up(p, b, j):
        single = (z == last - 1) & (p == 0) & (j >= 1) & (b != x)
        return (z < last) & (p <= z) & jnp.logical_not(single)

    def goes_x(p, b, j):
        return (z == last) & (p == 0) & (j >= 1) & (b == x)

    def send_own(j, carry):
        src = f_in.at[0, :, cols(j)]
        piece(own, j, xs_sem, x_id, src).start()

        @pl.when(z < last)
        def _():
            piece(own, j, up_sem, up_id, src).start()

        @pl.when(z > 0)
        def _():
            piece(own, j, dn_sem, dn_id, src).start()

        return carry

    lax.fori_loop(z, nz, send_own, 0)

    def krows(p):
        return pl.ds(pl.multiple_of(p * wide, 128), wide)

    def panel_chunk(p):
        return pltpu.make_async_remote_copy(
            src_ref=bp_in.at[0, krows(p), :],
            dst_ref=bp.at[x, krows(p), :],
            send_sem=bp_send.at[p],
            recv_sem=bp_recv.at[p],
            device_id=x_id,
            device_id_type=MESH,
        )

    def send_panel(e, carry):
        cp, cj = carry
        p, j = lax.rem(cp, nz), lax.rem(cj, nz)

        @pl.when(p == j)
        def _():
            panel_chunk(p).start()

        return cp // nz, cj // nz

    lax.fori_loop(0, count, send_panel, (code_p, code_j))

    acc[...] = jnp.zeros_like(acc)

    locals_[2].wait()
    locals_[1].wait()
    blocks = pat.shape[1]
    lane = wc // blocks

    @pl.loop(0, nz)
    def _(p):
        for t in range(pc // 256):
            r = pl.ds(pl.multiple_of(x * pc + t * 256, 128), 256)
            bt[r, cols(p)] = bp[x, krows(p), t * 256 : (t + 1) * 256].T
        for t in range(blocks):
            r = pl.ds(2 * pc + t * lane, lane)
            m = pat[0, t].astype(F32).astype(BF16)
            bt[r, cols(p)] = bw[krows(p), t * lane : (t + 1) * lane].T * m

    locals_[3].wait()
    locals_[4].wait()
    quarter = tot.shape[1]

    @pl.loop(0, 4)
    def _(q):
        c = pl.ds(pl.multiple_of(q * quarter, 128), quarter)
        tot[q] = -lax.dot_general(
            ep[:, c], er[...], (((0,), (0,)), ((), ())), preferred_element_type=F32
        )

    locals_[0].wait()
    locals_[5].wait()

    def accumulate(p, j, first, tiles):
        low = fg[2 * p, :, cols(j)]
        high = fg[2 * p + 1, :, cols(j)]
        right = jnp.concatenate([low, high], axis=0)
        for t in range(tiles):
            r = pl.ds(pl.multiple_of(first + t * 256, 128), 256)
            acc[r, cols(j)] += jnp.dot(bt[r, cols(p)], right, preferred_element_type=F32)

    def pass_on(p, b, j):
        d = 2 * p + b

        @pl.when((p != z) | (b != x))
        def _():
            piece(d, j, up_sem, up_id).wait_recv()

            @pl.when(goes_up(p, b, j))
            def _():
                piece(d, j, up_sem, up_id).start()

            @pl.when((z > 0) & (p >= z))
            def _():
                piece(d, j, dn_sem, dn_id).start()

            @pl.when(goes_x(p, b, j))
            def _():
                piece(d, j, xs_sem, x_id).start()

    lag = min(4, count - 1)

    def partner(p, j):
        @pl.when(p == j)
        def _():
            panel_chunk(p).wait_recv()
            for t in range(pc // 256):
                r = pl.ds(pl.multiple_of(ox * pc + t * 256, 128), 256)
                bt[r, cols(p)] = bp[ox, krows(p), t * 256 : (t + 1) * 256].T

        accumulate(p, j, ox * pc, pc // 256)

    def digits(cp, cj):
        return lax.rem(cp, nz), lax.rem(cj, nz)

    pass_on(*[v for v in (lax.rem(code_p, nz), x, lax.rem(code_j, nz))])

    def event(e, carry):
        cp, cj, lp, lj = carry
        p, j = digits(cp, cj)
        np_, nj = cp // nz, cj // nz

        @pl.when(e < count - 1)
        def _():
            a, b = digits(np_, nj)
            pass_on(a, x, b)

        pass_on(p, ox, j)
        accumulate(p, j, x * pc, pc // 256)
        accumulate(p, j, 2 * pc, wc // 256)
        late = e >= lag
        a, b = digits(lp, lj)

        @pl.when(late)
        def _():
            partner(a, b)

        return np_, nj, jnp.where(late, lp // nz, lp), jnp.where(late, lj // nz, lj)

    _, _, lp, lj = lax.fori_loop(0, count, event, (code_p, code_j, code_p, code_j))

    def rest(e, carry):
        lp, lj = carry
        a, b = digits(lp, lj)
        partner(a, b)
        return lp // nz, lj // nz

    lax.fori_loop(0, lag, rest, (lp, lj))

    window = acc[2 * pc : 2 * pc + wc, :].astype(BF16)

    def share(q):
        r = pl.ds(pl.multiple_of(q * quarter, 128), quarter)
        tot[q] += lax.dot_general(
            acc[r, :].astype(BF16), window, (((1,), (1,)), ((), ())), preferred_element_type=F32
        )

    def to_core(q, slot):
        return pltpu.make_async_remote_copy(
            src_ref=tot.at[q],
            dst_ref=half.at[slot],
            send_sem=c_send.at[slot],
            recv_sem=c_recv.at[slot],
            device_id={"grp": core},
            device_id_type=MESH,
        )

    first, second = to_core(3 - g, 0), to_core(core, 1)
    share(3 - g)
    first.start()
    share(core)
    second.start()
    share(far)
    first.wait_recv()
    ybuf[...] = (tot[far] + half[0]).astype(BF16)
    across = pltpu.make_async_remote_copy(
        src_ref=ybuf,
        dst_ref=yrecv,
        send_sem=y_send,
        recv_sem=y_recv,
        device_id={"grp": far},
        device_id_type=MESH,
    )
    across.start()
    share(g)
    second.wait_recv()
    mine = tot[g] + half[1]
    across.wait_recv()
    sch[g] = (mine + yrecv[...].astype(F32)).astype(BF16)

    def give(q, sems, slot, to):
        return pltpu.make_async_remote_copy(
            src_ref=sch.at[q],
            dst_ref=sch.at[q],
            send_sem=sems.at[slot],
            recv_sem=s_recv.at[q],
            device_id={"grp": to},
            device_id_type=MESH,
        )

    @pl.when(g < 2)
    def _():
        give(g, s_send, 0, far).start()

    @pl.when(lax.rem(g, 2) == 0)
    def _():
        give(g, s_send, 1, core).start()

    @pl.when(g >= 2)
    def _():
        give(far, s_fwd, 0, core).wait_recv()
        give(far, s_fwd, 0, core).start()

    def part(q):
        c = pl.ds(pl.multiple_of(q * quarter, 128), quarter)
        return jnp.dot(pv[:, c], sch[q], preferred_element_type=F32)

    res = half.at[0]
    res[...] = part(g)

    @pl.when(g >= 2)
    def _():
        res[...] += part(far)

    @pl.when(lax.rem(g, 2) == 1)
    def _():
        give(core, s_fwd, 0, core).wait_recv()
        res[...] += part(core)

    @pl.when(g >= 2)
    def _():
        give(3 - g, s_fwd, 0, core).wait_recv()
        res[...] += part(3 - g)

    out[...] = res[...].astype(out.dtype)

    first.wait_send()
    second.wait_send()
    across.wait_send()

    @pl.when(g < 2)
    def _():
        give(g, s_send, 0, far).wait_send()

    @pl.when(lax.rem(g, 2) == 0)
    def _():
        give(g, s_send, 1, core).wait_send()

    @pl.when(g >= 2)
    def _():
        give(far, s_fwd, 0, core).wait_send()

    def drain(e, carry):
        cp, cj = carry
        p, j = digits(cp, cj)

        @pl.when(p == j)
        def _():
            panel_chunk(p).wait_send()

        for b in range(2):
            d = 2 * p + b

            @pl.when(goes_up(p, b, j))
            def _():
                piece(d, j, up_sem, up_id).wait_send()

            @pl.when((z > 0) & (p >= z))
            def _():
                piece(d, j, dn_sem, dn_id).wait_send()

            @pl.when(goes_x(p, b, j) | ((p == z) & (b == x)))
            def _():
                piece(d, j, xs_sem, x_id).wait_send()

        return cp // nz, cj // nz

    lax.fori_loop(0, count, drain, (code_p, code_j))


def fused(nz):
    def run(f, bw, bp, pat, er, ep, pv):
        rows, order = f.shape[1:]
        pc, wc, total = bp.shape[2], bw.shape[2], ep.shape[1]
        dma = pltpu.SemaphoreType.DMA
        anywhere = pl.BlockSpec(memory_space=pl.ANY)
        return pl.pallas_call(
            functools.partial(panel_kernel, nz),
            out_shape=jax.ShapeDtypeStruct((pv.shape[0], wc), BF16),
            in_specs=[anywhere] * 3
            + [pl.BlockSpec(memory_space=pltpu.SMEM)]
            + [anywhere] * 3,
            out_specs=pl.BlockSpec(memory_space=pltpu.VMEM),
            scratch_shapes=[
                pltpu.VMEM((2 * nz, rows, order), BF16),
                pltpu.VMEM((order, wc), BF16),
                pltpu.VMEM((2, order, pc), BF16),
                pltpu.VMEM(er.shape, BF16),
                pltpu.VMEM(ep.shape, BF16),
                pltpu.VMEM(pv.shape, BF16),
                pltpu.VMEM((2 * pc + wc, order), BF16),
                pltpu.VMEM((2 * pc + wc, order), F32),
                pltpu.VMEM((4, total // 4, wc), F32),
                pltpu.VMEM((2, total // 4, wc), F32),
                pltpu.VMEM((total // 4, wc), BF16),
                pltpu.VMEM((total // 4, wc), BF16),
                pltpu.VMEM((4, total // 4, wc), BF16),
                dma((6,)),
                dma((2 * nz, nz)),
                dma((2 * nz, nz)),
                dma((2 * nz, nz)),
                dma((2 * nz, nz)),
                dma((nz,)),
                dma((nz,)),
                dma((2,)),
                dma((2,)),
                dma,
                dma,
                dma((2,)),
                dma((1,)),
                dma((4,)),
            ],
            compiler_params=pltpu.CompilerParams(
                collective_id=0, has_side_effects=True, vmem_limit_bytes=60 * 2**20
            ),
        )(f, bw, bp, pat, er, ep, pv)

    return run


def fits(mesh, f, bw, bp, pat, er, ep, pv):
    nz = mesh.shape["scen"]
    order = f.shape[2]
    return (
        mesh.shape["slab"] == 2
        and mesh.shape["grp"] == 4
        and nz >= 2
        and order % (128 * nz) == 0
        and f.shape[1] * 2 * nz == order
        and f.shape[1] % 16 == 0
        and bw.shape[2] % 256 == 0
        and bp.shape[2] % 256 == 0
        and ep.shape[1] == 2 * bp.shape[2]
        and ep.shape[1] % 512 == 0
        and pv.shape[0] * 4 == ep.shape[1]
        and (bw.shape[2] // pat.shape[1]) % 128 == 0
        and nz ** (nz * (nz + 1) // 2) < 2**31
    )


def body(
    factor_inverse,
    border_window,
    border_panel,
    border_pattern,
    earlier_rows,
    earlier_panel,
    pivot_inverse,
):
    window = border_window[0]
    columns = window.shape[1]
    blocks = border_pattern.shape[1]
    column_mask = jnp.repeat(border_pattern[0].astype(jnp.bfloat16), columns // blocks)
    masked = window * column_mask[None, :]
    panel_border = border_panel[0]
    incoming = lax.all_gather(factor_inverse[0], ("scen", "slab"), axis=0, tiled=True)
    window_sum = lax.dot_general(
        incoming, masked, (((0,), (0,)), ((), ())), preferred_element_type=jnp.float32
    )
    panel_sum = lax.dot_general(
        panel_border, incoming, (((0,), (0,)), ((), ())), preferred_element_type=jnp.float32
    )
    window_sum, panel_sum = (window_sum, panel_sum)
    window_image = window_sum.astype(jnp.bfloat16)
    panel_piece = panel_sum.astype(jnp.bfloat16)
    panel_image = lax.all_gather(panel_piece, "slab", axis=0, tiled=True)
    contribution = jnp.dot(panel_image, window_image, preferred_element_type=jnp.float32)
    update = lax.dot_general(
        earlier_panel, earlier_rows, (((0,), (0,)), ((), ())), preferred_element_type=jnp.float32
    )
    partial_sum = contribution - update
    schur_block = lax.psum(partial_sum, "grp").astype(jnp.bfloat16)
    return jnp.dot(pivot_inverse, schur_block, preferred_element_type=jnp.float32).astype(
        jnp.bfloat16
    )


def solution(mesh):
    placed = (
        P("grp", ("scen", "slab"), None),
        P("grp", None, ("scen", "slab")),
        P("grp", None, "slab"),
        P("grp", ("scen", "slab")),
        P("grp", ("scen", "slab")),
        P("grp", None),
        P("grp", None),
    )

    def either(*blocks):
        if fits(mesh, *blocks):
            return fused(mesh.shape["scen"])(*blocks)
        return body(*blocks)

    return jax.shard_map(
        either, mesh=mesh, in_specs=placed, out_specs=P("grp", ("scen", "slab")), check_vma=False
    )
```

```python
import functools

import jax
import jax.numpy as jnp
from jax import lax
from jax.experimental import pallas as pl
from jax.experimental.pallas import tpu as pltpu
from jax.sharding import PartitionSpec as P


F32 = jnp.float32
BF16 = jnp.bfloat16
MESH = pl.DeviceIdType.MESH


def event_codes(nz):
    codes = []
    for z in range(nz):
        pairs = sorted(range(nz), key=lambda p: (abs(p - z), p < z))
        events = [(p, j) for p in pairs for j in range(p, nz)]
        codes.append(
            (
                sum(p * nz**e for e, (p, j) in enumerate(events)),
                sum(j * nz**e for e, (p, j) in enumerate(events)),
            )
        )
    return codes


def pick(index, values):
    chosen = jnp.int32(values[0])
    for i, value in enumerate(values[1:], 1):
        chosen = jnp.where(index == i, jnp.int32(value), chosen)
    return chosen


def panel_kernel(
    nz,
    f_in,
    bw_in,
    bp_in,
    pat,
    er_in,
    ep_in,
    pv_in,
    out,
    fg,
    bw,
    bp,
    er,
    ep,
    pv,
    bt,
    acc,
    tot,
    half,
    ybuf,
    yrecv,
    sch,
    loc_sem,
    f_recv,
    up_sem,
    dn_sem,
    xs_sem,
    bp_send,
    bp_recv,
    c_send,
    c_recv,
    y_send,
    y_recv,
    s_send,
    s_fwd,
    s_recv,
):
    z = lax.axis_index("scen")
    x = lax.axis_index("slab")
    g = lax.axis_index("grp")
    ox = 1 - x
    core = g + 1 - 2 * lax.rem(g, 2)
    far = lax.rem(g + 2, 4)
    last = nz - 1
    rows = f_in.shape[1]
    order = f_in.shape[2]
    wide = order // nz
    pc = bp_in.shape[2]
    wc = bw_in.shape[2]
    count = nz * (nz + 1) // 2
    codes = event_codes(nz)
    code_p = pick(z, [c[0] for c in codes])
    code_j = pick(z, [c[1] for c in codes])
    up_id, dn_id, x_id = {"scen": z + 1}, {"scen": z - 1}, {"slab": ox}

    own = 2 * z + x
    locals_ = [
        pltpu.make_async_copy(f_in.at[0], fg.at[own], loc_sem.at[0]),
        pltpu.make_async_copy(bw_in.at[0], bw, loc_sem.at[1]),
        pltpu.make_async_copy(bp_in.at[0], bp.at[x], loc_sem.at[2]),
        pltpu.make_async_copy(er_in, er, loc_sem.at[3]),
        pltpu.make_async_copy(ep_in, ep, loc_sem.at[4]),
        pltpu.make_async_copy(pv_in, pv, loc_sem.at[5]),
    ]
    for c in locals_:
        c.start()

    cut = rows // 128 * 128
    for p in range(nz if cut else 0):

        @pl.when(z != p)
        def _():
            fg[2 * p + 1, :, p * wide : p * wide + cut] = jnp.zeros((rows, cut), BF16)

    barrier = pltpu.get_barrier_semaphore()

    @pl.when(z < last)
    def _():
        pl.semaphore_signal(barrier, inc=1, device_id=up_id, device_id_type=MESH)

    @pl.when(z > 0)
    def _():
        pl.semaphore_signal(barrier, inc=1, device_id=dn_id, device_id_type=MESH)

    for peer in (x_id, {"grp": core}, {"grp": far}):
        pl.semaphore_signal(barrier, inc=1, device_id=peer, device_id_type=MESH)
    pl.semaphore_wait(barrier, 3 + jnp.where(z < last, 1, 0) + jnp.where(z > 0, 1, 0))

    def cols(j):
        return pl.ds(pl.multiple_of(j * wide, 128), wide)

    def piece(action, p, b, j, sems, peer, input_block=False):
        d = 2 * p + b
        short = (p == j) & (b == 1)

        def copy(skip):
            c = pl.ds(pl.multiple_of(j * wide + skip, 128), wide - skip)
            here = fg.at[d, :, c]
            getattr(
                pltpu.make_async_remote_copy(
                    src_ref=f_in.at[0, :, c] if input_block else here,
                    dst_ref=here,
                    send_sem=sems.at[d, j],
                    recv_sem=f_recv.at[d, j],
                    device_id=peer,
                    device_id_type=MESH,
                ),
                action,
            )()

        @pl.when(short)
        def _():
            copy(cut)

        @pl.when(jnp.logical_not(short))
        def _():
            copy(0)

    def alone(to, p, j):
        return (to == last) & (p == 0) & (j < last)

    def goes_up(p, b, j):
        return (z < last) & (p <= z) & jnp.logical_not(alone(z + 1, p, j) & (b != x))

    def goes_x(p, b, j):
        return alone(z, p, j) & (b == x)

    def send_own(j, carry):
        piece("start", z, x, j, xs_sem, x_id, True)

        @pl.when(z < last)
        def _():
            piece("start", z, x, j, up_sem, up_id, True)

        @pl.when(z > 0)
        def _():
            piece("start", z, x, j, dn_sem, dn_id, True)

        return carry

    lax.fori_loop(z, nz, send_own, 0)

    def krows(p):
        return pl.ds(pl.multiple_of(p * wide, 128), wide)

    def panel_chunk(p):
        return pltpu.make_async_remote_copy(
            src_ref=bp_in.at[0, krows(p), :],
            dst_ref=bp.at[x, krows(p), :],
            send_sem=bp_send.at[p],
            recv_sem=bp_recv.at[p],
            device_id=x_id,
            device_id_type=MESH,
        )

    def send_panel(e, carry):
        cp, cj = carry
        p, j = lax.rem(cp, nz), lax.rem(cj, nz)

        @pl.when(p == j)
        def _():
            panel_chunk(p).start()

        return cp // nz, cj // nz

    lax.fori_loop(0, count, send_panel, (code_p, code_j))

    acc[...] = jnp.zeros_like(acc)

    locals_[2].wait()
    locals_[1].wait()
    blocks = pat.shape[1]
    lane = wc // blocks

    @pl.loop(0, nz)
    def _(p):
        for t in range(pc // 256):
            r = pl.ds(pl.multiple_of(x * pc + t * 256, 128), 256)
            bt[r, cols(p)] = bp[x, krows(p), t * 256 : (t + 1) * 256].T
        for t in range(blocks):
            r = pl.ds(2 * pc + t * lane, lane)
            m = pat[0, t].astype(F32).astype(BF16)
            bt[r, cols(p)] = bw[krows(p), t * lane : (t + 1) * lane].T * m

    locals_[3].wait()
    locals_[4].wait()
    quarter = tot.shape[1]

    @pl.loop(0, 4)
    def _(q):
        c = pl.ds(pl.multiple_of(q * quarter, 128), quarter)
        tot[q] = -lax.dot_general(
            ep[:, c], er[...], (((0,), (0,)), ((), ())), preferred_element_type=F32
        )

    locals_[0].wait()
    locals_[5].wait()

    def accumulate(p, j, first, tiles):
        low = fg[2 * p, :, cols(j)]
        high = fg[2 * p + 1, :, cols(j)]
        right = jnp.concatenate([low, high], axis=0)
        for t in range(tiles):
            r = pl.ds(pl.multiple_of(first + t * 256, 128), 256)
            acc[r, cols(j)] += jnp.dot(bt[r, cols(p)], right, preferred_element_type=F32)

    def pass_on(p, b, j):
        @pl.when((p != z) | (b != x))
        def _():
            piece("wait_recv", p, b, j, up_sem, up_id)

            @pl.when(goes_up(p, b, j))
            def _():
                piece("start", p, b, j, up_sem, up_id)

            @pl.when((z > 0) & (p >= z))
            def _():
                piece("start", p, b, j, dn_sem, dn_id)

            @pl.when(goes_x(p, b, j))
            def _():
                piece("start", p, b, j, xs_sem, x_id)

    def partner(p, j):
        @pl.when(p == j)
        def _():
            panel_chunk(p).wait_recv()
            for t in range(pc // 256):
                r = pl.ds(pl.multiple_of(ox * pc + t * 256, 128), 256)
                bt[r, cols(p)] = bp[ox, krows(p), t * 256 : (t + 1) * 256].T

        accumulate(p, j, ox * pc, pc // 256)

    def digits(cp, cj):
        return lax.rem(cp, nz), lax.rem(cj, nz)

    pass_on(*[v for v in (lax.rem(code_p, nz), x, lax.rem(code_j, nz))])

    def due(e):
        behind = jnp.where((z == last) & (e >= count - nz), e, jnp.maximum(e - 3, 0))
        return jnp.where(e == count - 1, count, behind)

    def late(i, carry):
        lp, lj = carry
        partner(*digits(lp, lj))
        return lp // nz, lj // nz

    def event(e, carry):
        cp, cj, done, lp, lj = carry
        p, j = digits(cp, cj)
        np_, nj = cp // nz, cj // nz

        @pl.when(e < count - 1)
        def _():
            a, b = digits(np_, nj)
            pass_on(a, x, b)

        pass_on(p, ox, j)
        accumulate(p, j, x * pc, pc // 256)
        accumulate(p, j, 2 * pc, wc // 256)
        target = due(e)
        lp, lj = lax.fori_loop(done, target, late, (lp, lj))
        return np_, nj, target, lp, lj

    lax.fori_loop(0, count, event, (code_p, code_j, jnp.int32(0), code_p, code_j))

    window = acc[2 * pc : 2 * pc + wc, :].astype(BF16)

    def share(q):
        r = pl.ds(pl.multiple_of(q * quarter, 128), quarter)
        tot[q] += lax.dot_general(
            acc[r, :].astype(BF16), window, (((1,), (1,)), ((), ())), preferred_element_type=F32
        )

    def to_core(q, slot):
        return pltpu.make_async_remote_copy(
            src_ref=tot.at[q],
            dst_ref=half.at[slot],
            send_sem=c_send.at[slot],
            recv_sem=c_recv.at[slot],
            device_id={"grp": core},
            device_id_type=MESH,
        )

    first, second = to_core(3 - g, 0), to_core(core, 1)
    share(3 - g)
    first.start()
    share(core)
    second.start()
    share(far)
    first.wait_recv()
    ybuf[...] = (tot[far] + half[0]).astype(BF16)
    across = pltpu.make_async_remote_copy(
        src_ref=ybuf,
        dst_ref=yrecv,
        send_sem=y_send,
        recv_sem=y_recv,
        device_id={"grp": far},
        device_id_type=MESH,
    )
    across.start()
    share(g)
    second.wait_recv()
    mine = tot[g] + half[1]
    across.wait_recv()
    sch[g] = (mine + yrecv[...].astype(F32)).astype(BF16)

    def give(q, sems, slot, to):
        return pltpu.make_async_remote_copy(
            src_ref=sch.at[q],
            dst_ref=sch.at[q],
            send_sem=sems.at[slot],
            recv_sem=s_recv.at[q],
            device_id={"grp": to},
            device_id_type=MESH,
        )

    @pl.when(g < 2)
    def _():
        give(g, s_send, 0, far).start()

    @pl.when(lax.rem(g, 2) == 0)
    def _():
        give(g, s_send, 1, core).start()

    @pl.when(g >= 2)
    def _():
        give(far, s_fwd, 0, core).wait_recv()
        give(far, s_fwd, 0, core).start()

    def part(q):
        c = pl.ds(pl.multiple_of(q * quarter, 128), quarter)
        return jnp.dot(pv[:, c], sch[q], preferred_element_type=F32)

    res = half.at[0]
    res[...] = part(g)

    @pl.when(g >= 2)
    def _():
        res[...] += part(far)

    @pl.when(lax.rem(g, 2) == 1)
    def _():
        give(core, s_fwd, 0, core).wait_recv()
        res[...] += part(core)

    @pl.when(g >= 2)
    def _():
        give(3 - g, s_fwd, 0, core).wait_recv()
        res[...] += part(3 - g)

    out[...] = res[...].astype(out.dtype)

    first.wait_send()
    second.wait_send()
    across.wait_send()

    @pl.when(g < 2)
    def _():
        give(g, s_send, 0, far).wait_send()

    @pl.when(lax.rem(g, 2) == 0)
    def _():
        give(g, s_send, 1, core).wait_send()

    @pl.when(g >= 2)
    def _():
        give(far, s_fwd, 0, core).wait_send()

    def drain(e, carry):
        cp, cj = carry
        p, j = digits(cp, cj)

        @pl.when(p == j)
        def _():
            panel_chunk(p).wait_send()

        for b in range(2):
            @pl.when(goes_up(p, b, j))
            def _():
                piece("wait_send", p, b, j, up_sem, up_id)

            @pl.when((z > 0) & (p >= z))
            def _():
                piece("wait_send", p, b, j, dn_sem, dn_id)

            @pl.when(goes_x(p, b, j) | ((p == z) & (b == x)))
            def _():
                piece("wait_send", p, b, j, xs_sem, x_id)

        return cp // nz, cj // nz

    lax.fori_loop(0, count, drain, (code_p, code_j))


def fused(nz):
    def run(f, bw, bp, pat, er, ep, pv):
        rows, order = f.shape[1:]
        pc, wc, total = bp.shape[2], bw.shape[2], ep.shape[1]
        dma = pltpu.SemaphoreType.DMA
        anywhere = pl.BlockSpec(memory_space=pl.ANY)
        return pl.pallas_call(
            functools.partial(panel_kernel, nz),
            out_shape=jax.ShapeDtypeStruct((pv.shape[0], wc), BF16),
            in_specs=[anywhere] * 3
            + [pl.BlockSpec(memory_space=pltpu.SMEM)]
            + [anywhere] * 3,
            out_specs=pl.BlockSpec(memory_space=pltpu.VMEM),
            scratch_shapes=[
                pltpu.VMEM((2 * nz, rows, order), BF16),
                pltpu.VMEM((order, wc), BF16),
                pltpu.VMEM((2, order, pc), BF16),
                pltpu.VMEM(er.shape, BF16),
                pltpu.VMEM(ep.shape, BF16),
                pltpu.VMEM(pv.shape, BF16),
                pltpu.VMEM((2 * pc + wc, order), BF16),
                pltpu.VMEM((2 * pc + wc, order), F32),
                pltpu.VMEM((4, total // 4, wc), F32),
                pltpu.VMEM((2, total // 4, wc), F32),
                pltpu.VMEM((total // 4, wc), BF16),
                pltpu.VMEM((total // 4, wc), BF16),
                pltpu.VMEM((4, total // 4, wc), BF16),
                dma((6,)),
                dma((2 * nz, nz)),
                dma((2 * nz, nz)),
                dma((2 * nz, nz)),
                dma((2 * nz, nz)),
                dma((nz,)),
                dma((nz,)),
                dma((2,)),
                dma((2,)),
                dma,
                dma,
                dma((2,)),
                dma((1,)),
                dma((4,)),
            ],
            compiler_params=pltpu.CompilerParams(
                collective_id=0, has_side_effects=True, vmem_limit_bytes=60 * 2**20
            ),
        )(f, bw, bp, pat, er, ep, pv)

    return run


def fits(mesh, f, bw, bp, pat, er, ep, pv):
    nz = mesh.shape["scen"]
    order = f.shape[2]
    return (
        mesh.shape["slab"] == 2
        and mesh.shape["grp"] == 4
        and nz >= 2
        and order % (128 * nz) == 0
        and f.shape[1] * 2 * nz == order
        and f.shape[1] % 16 == 0
        and bw.shape[2] % 256 == 0
        and bp.shape[2] % 256 == 0
        and ep.shape[1] == 2 * bp.shape[2]
        and ep.shape[1] % 512 == 0
        and pv.shape[0] * 4 == ep.shape[1]
        and (bw.shape[2] // pat.shape[1]) % 128 == 0
        and nz ** (nz * (nz + 1) // 2) < 2**31
    )


def body(
    factor_inverse,
    border_window,
    border_panel,
    border_pattern,
    earlier_rows,
    earlier_panel,
    pivot_inverse,
):
    window = border_window[0]
    columns = window.shape[1]
    blocks = border_pattern.shape[1]
    column_mask = jnp.repeat(border_pattern[0].astype(jnp.bfloat16), columns // blocks)
    masked = window * column_mask[None, :]
    panel_border = border_panel[0]
    incoming = lax.all_gather(factor_inverse[0], ("scen", "slab"), axis=0, tiled=True)
    window_sum = lax.dot_general(
        incoming, masked, (((0,), (0,)), ((), ())), preferred_element_type=jnp.float32
    )
    panel_sum = lax.dot_general(
        panel_border, incoming, (((0,), (0,)), ((), ())), preferred_element_type=jnp.float32
    )
    window_sum, panel_sum = (window_sum, panel_sum)
    window_image = window_sum.astype(jnp.bfloat16)
    panel_piece = panel_sum.astype(jnp.bfloat16)
    panel_image = lax.all_gather(panel_piece, "slab", axis=0, tiled=True)
    contribution = jnp.dot(panel_image, window_image, preferred_element_type=jnp.float32)
    update = lax.dot_general(
        earlier_panel, earlier_rows, (((0,), (0,)), ((), ())), preferred_element_type=jnp.float32
    )
    partial_sum = contribution - update
    schur_block = lax.psum(partial_sum, "grp").astype(jnp.bfloat16)
    return jnp.dot(pivot_inverse, schur_block, preferred_element_type=jnp.float32).astype(
        jnp.bfloat16
    )


def solution(mesh):
    placed = (
        P("grp", ("scen", "slab"), None),
        P("grp", None, ("scen", "slab")),
        P("grp", None, "slab"),
        P("grp", ("scen", "slab")),
        P("grp", ("scen", "slab")),
        P("grp", None),
        P("grp", None),
    )

    def either(*blocks):
        if fits(mesh, *blocks):
            return fused(mesh.shape["scen"])(*blocks)
        return body(*blocks)

    return jax.shard_map(
        either, mesh=mesh, in_specs=placed, out_specs=P("grp", ("scen", "slab")), check_vma=False
    )
```

```python
import functools

import jax
import jax.numpy as jnp
from jax import lax
from jax.experimental import pallas as pl
from jax.experimental.pallas import tpu as pltpu
from jax.sharding import PartitionSpec as P


F32 = jnp.float32
BF16 = jnp.bfloat16
MESH = pl.DeviceIdType.MESH


def event_codes(nz):
    codes = []
    for z in range(nz):
        pairs = sorted(range(nz), key=lambda p: (abs(p - z), p < z))
        events = [(p, j) for p in pairs for j in range(p, nz)]
        codes.append(
            (
                sum(p * nz**e for e, (p, j) in enumerate(events)),
                sum(j * nz**e for e, (p, j) in enumerate(events)),
            )
        )
    return codes


def diagonal_steps(rows):
    steps = []
    for b in range(2):
        base = b * rows
        skip = base // 128 * 128
        edge = skip + 128 - base
        if edge < rows and edge % 16 == 0:
            steps.append([(0, edge, skip), (edge, rows - edge, skip + 128)])
        else:
            steps.append([(0, rows, skip)])
    return steps


def pick(index, values):
    chosen = jnp.int32(values[0])
    for i, value in enumerate(values[1:], 1):
        chosen = jnp.where(index == i, jnp.int32(value), chosen)
    return chosen


def panel_kernel(
    nz,
    f_in,
    bw_in,
    bp_in,
    pat,
    er_in,
    ep_in,
    pv_in,
    out,
    fg,
    bw,
    bp,
    er,
    ep,
    pv,
    bt,
    acc,
    tot,
    half,
    ybuf,
    yrecv,
    sch,
    loc_sem,
    f_recv,
    up_sem,
    dn_sem,
    xs_sem,
    bp_send,
    bp_recv,
    c_send,
    c_recv,
    y_send,
    y_recv,
    s_send,
    s_fwd,
    s_recv,
):
    z = lax.axis_index("scen")
    x = lax.axis_index("slab")
    g = lax.axis_index("grp")
    ox = 1 - x
    core = g + 1 - 2 * lax.rem(g, 2)
    far = lax.rem(g + 2, 4)
    last = nz - 1
    rows = f_in.shape[1]
    order = f_in.shape[2]
    wide = order // nz
    pc = bp_in.shape[2]
    wc = bw_in.shape[2]
    count = nz * (nz + 1) // 2
    codes = event_codes(nz)
    code_p = pick(z, [c[0] for c in codes])
    code_j = pick(z, [c[1] for c in codes])
    up_id, dn_id, x_id = {"scen": z + 1}, {"scen": z - 1}, {"slab": ox}

    own = 2 * z + x
    locals_ = [
        pltpu.make_async_copy(f_in.at[0], fg.at[own], loc_sem.at[0]),
        pltpu.make_async_copy(bw_in.at[0], bw, loc_sem.at[1]),
        pltpu.make_async_copy(bp_in.at[0], bp.at[x], loc_sem.at[2]),
        pltpu.make_async_copy(er_in, er, loc_sem.at[3]),
        pltpu.make_async_copy(ep_in, ep, loc_sem.at[4]),
        pltpu.make_async_copy(pv_in, pv, loc_sem.at[5]),
    ]
    for c in locals_:
        c.start()

    steps = diagonal_steps(rows)
    for p in range(nz):

        @pl.when(z != p)
        def _():
            for b, parts in enumerate(steps):
                for first, height, skip in parts:
                    if skip:
                        gap = fg.at[2 * p + b, first : first + height, p * wide : p * wide + skip]
                        gap[...] = jnp.zeros(gap.shape, BF16)

    barrier = pltpu.get_barrier_semaphore()

    @pl.when(z < last)
    def _():
        pl.semaphore_signal(barrier, inc=1, device_id=up_id, device_id_type=MESH)

    @pl.when(z > 0)
    def _():
        pl.semaphore_signal(barrier, inc=1, device_id=dn_id, device_id_type=MESH)

    for peer in (x_id, {"grp": core}, {"grp": far}):
        pl.semaphore_signal(barrier, inc=1, device_id=peer, device_id_type=MESH)
    pl.semaphore_wait(barrier, 3 + jnp.where(z < last, 1, 0) + jnp.where(z > 0, 1, 0))

    def cols(j):
        return pl.ds(pl.multiple_of(j * wide, 128), wide)

    def piece(action, p, b, j, sems, peer, input_block=False):
        d = 2 * p + b

        def copy(index, first, height, skip):
            c = pl.ds(pl.multiple_of(j * wide + skip, 128), wide - skip)
            r = pl.ds(first, height)
            here = fg.at[d, r, c]
            getattr(
                pltpu.make_async_remote_copy(
                    src_ref=f_in.at[0, r, c] if input_block else here,
                    dst_ref=here,
                    send_sem=sems.at[d, j + index],
                    recv_sem=f_recv.at[d, j + index],
                    device_id=peer,
                    device_id_type=MESH,
                ),
                action,
            )()

        for half_block, parts in enumerate(steps):

            @pl.when((p == j) & (b == half_block))
            def _():
                for index, part in enumerate(parts):
                    copy(index * (nz - j), *part)

        @pl.when(p != j)
        def _():
            copy(0, 0, rows, 0)

    def alone(to, p, j):
        return (to == last) & (p == 0) & (2 * j < nz)

    def goes_up(p, b, j):
        return (z < last) & (p <= z) & jnp.logical_not(alone(z + 1, p, j) & (b != x))

    def goes_x(p, b, j):
        return alone(z, p, j) & (b == x)

    def send_own(j, carry):
        piece("start", z, x, j, xs_sem, x_id, True)

        @pl.when(z < last)
        def _():
            piece("start", z, x, j, up_sem, up_id, True)

        @pl.when(z > 0)
        def _():
            piece("start", z, x, j, dn_sem, dn_id, True)

        return carry

    lax.fori_loop(z, nz, send_own, 0)

    def krows(p):
        return pl.ds(pl.multiple_of(p * wide, 128), wide)

    def panel_chunk(p):
        return pltpu.make_async_remote_copy(
            src_ref=bp_in.at[0, krows(p), :],
            dst_ref=bp.at[x, krows(p), :],
            send_sem=bp_send.at[p],
            recv_sem=bp_recv.at[p],
            device_id=x_id,
            device_id_type=MESH,
        )

    def send_panel(e, carry):
        cp, cj = carry
        p, j = lax.rem(cp, nz), lax.rem(cj, nz)

        @pl.when(p == j)
        def _():
            panel_chunk(p).start()

        return cp // nz, cj // nz

    lax.fori_loop(0, count, send_panel, (code_p, code_j))

    acc[...] = jnp.zeros_like(acc)

    locals_[2].wait()
    locals_[1].wait()
    blocks = pat.shape[1]
    lane = wc // blocks

    @pl.loop(0, nz)
    def _(p):
        for t in range(pc // 256):
            r = pl.ds(pl.multiple_of(x * pc + t * 256, 128), 256)
            bt[r, cols(p)] = bp[x, krows(p), t * 256 : (t + 1) * 256].T
        for t in range(blocks):
            r = pl.ds(2 * pc + t * lane, lane)
            m = pat[0, t].astype(F32).astype(BF16)
            bt[r, cols(p)] = bw[krows(p), t * lane : (t + 1) * lane].T * m

    locals_[3].wait()
    locals_[4].wait()
    quarter = tot.shape[1]

    @pl.loop(0, 4)
    def _(q):
        c = pl.ds(pl.multiple_of(q * quarter, 128), quarter)
        tot[q] = -lax.dot_general(
            ep[:, c], er[...], (((0,), (0,)), ((), ())), preferred_element_type=F32
        )

    locals_[0].wait()
    locals_[5].wait()

    def accumulate(p, j, first, tiles):
        low = fg[2 * p, :, cols(j)]
        high = fg[2 * p + 1, :, cols(j)]
        right = jnp.concatenate([low, high], axis=0)
        for t in range(tiles):
            r = pl.ds(pl.multiple_of(first + t * 256, 128), 256)
            acc[r, cols(j)] += jnp.dot(bt[r, cols(p)], right, preferred_element_type=F32)

    def pass_on(p, b, j):
        @pl.when((p != z) | (b != x))
        def _():
            piece("wait_recv", p, b, j, up_sem, up_id)

            @pl.when(goes_up(p, b, j))
            def _():
                piece("start", p, b, j, up_sem, up_id)

            @pl.when((z > 0) & (p >= z))
            def _():
                piece("start", p, b, j, dn_sem, dn_id)

            @pl.when(goes_x(p, b, j))
            def _():
                piece("start", p, b, j, xs_sem, x_id)

    def partner(p, j):
        @pl.when(p == j)
        def _():
            panel_chunk(p).wait_recv()
            for t in range(pc // 256):
                r = pl.ds(pl.multiple_of(ox * pc + t * 256, 128), 256)
                bt[r, cols(p)] = bp[ox, krows(p), t * 256 : (t + 1) * 256].T

        accumulate(p, j, ox * pc, pc // 256)

    def digits(cp, cj):
        return lax.rem(cp, nz), lax.rem(cj, nz)

    pass_on(*[v for v in (lax.rem(code_p, nz), x, lax.rem(code_j, nz))])

    def due(e):
        behind = jnp.where((z == last) & (e >= count - nz), e, jnp.maximum(e - 3, 0))
        return jnp.where(e == count - 1, count, behind)

    def late(i, carry):
        lp, lj = carry
        partner(*digits(lp, lj))
        return lp // nz, lj // nz

    def event(e, carry):
        cp, cj, done, lp, lj = carry
        p, j = digits(cp, cj)
        np_, nj = cp // nz, cj // nz

        @pl.when(e < count - 1)
        def _():
            a, b = digits(np_, nj)
            pass_on(a, x, b)

        pass_on(p, ox, j)
        accumulate(p, j, x * pc, pc // 256)
        accumulate(p, j, 2 * pc, wc // 256)
        target = due(e)
        lp, lj = lax.fori_loop(done, target, late, (lp, lj))
        return np_, nj, target, lp, lj

    lax.fori_loop(0, count, event, (code_p, code_j, jnp.int32(0), code_p, code_j))

    window = acc[2 * pc : 2 * pc + wc, :].astype(BF16)

    def share(q):
        r = pl.ds(pl.multiple_of(q * quarter, 128), quarter)
        tot[q] += lax.dot_general(
            acc[r, :].astype(BF16), window, (((1,), (1,)), ((), ())), preferred_element_type=F32
        )

    def to_core(q, slot, r):
        return pltpu.make_async_remote_copy(
            src_ref=tot.at[q, r, :],
            dst_ref=half.at[min(slot, 2) // 2, r, :],
            send_sem=c_send.at[slot],
            recv_sem=c_recv.at[slot],
            device_id={"grp": core},
            device_id_type=MESH,
        )

    mid = quarter // 2
    halves = [pl.ds(0, mid), pl.ds(mid, mid)]
    first = [to_core(3 - g, h, r) for h, r in enumerate(halves)]
    second = to_core(core, 2, pl.ds(0, quarter))
    across = [
        pltpu.make_async_remote_copy(
            src_ref=ybuf.at[r, :],
            dst_ref=yrecv.at[r, :],
            send_sem=y_send.at[h],
            recv_sem=y_recv.at[h],
            device_id={"grp": far},
            device_id_type=MESH,
        )
        for h, r in enumerate(halves)
    ]

    def give(q, h, sems, slot, to):
        here = sch.at[q, halves[h], :]
        return pltpu.make_async_remote_copy(
            src_ref=here,
            dst_ref=here,
            send_sem=sems.at[slot, h],
            recv_sem=s_recv.at[q, h],
            device_id={"grp": to},
            device_id_type=MESH,
        )

    share(3 - g)
    for c in first:
        c.start()
    share(core)
    second.start()
    share(far)
    for h, r in enumerate(halves):
        first[h].wait_recv()
        ybuf[r, :] = (tot[far, r, :] + half[0, r, :]).astype(BF16)
        across[h].start()
    share(g)
    second.wait_recv()
    for h, r in enumerate(halves):
        across[h].wait_recv()
        sch[g, r, :] = (tot[g, r, :] + half[1, r, :] + yrecv[r, :].astype(F32)).astype(BF16)

        @pl.when(g < 2)
        def _():
            give(g, h, s_send, 0, far).start()

        @pl.when(lax.rem(g, 2) == 0)
        def _():
            give(g, h, s_send, 1, core).start()

    def part(q):
        c = pl.ds(pl.multiple_of(q * quarter, 128), quarter)
        return jnp.dot(pv[:, c], sch[q], preferred_element_type=F32)

    res = half.at[0]
    res[...] = part(g)

    @pl.when(g >= 2)
    def _():
        for h in range(2):
            give(far, h, s_fwd, 0, core).wait_recv()
            give(far, h, s_fwd, 0, core).start()
        res[...] += part(far)

    @pl.when(lax.rem(g, 2) == 1)
    def _():
        for h in range(2):
            give(core, h, s_fwd, 0, core).wait_recv()
        res[...] += part(core)

    @pl.when(g >= 2)
    def _():
        for h in range(2):
            give(3 - g, h, s_fwd, 0, core).wait_recv()
        res[...] += part(3 - g)

    out[...] = res[...].astype(out.dtype)

    second.wait_send()
    for h in range(2):
        first[h].wait_send()
        across[h].wait_send()

        @pl.when(g < 2)
        def _():
            give(g, h, s_send, 0, far).wait_send()

        @pl.when(lax.rem(g, 2) == 0)
        def _():
            give(g, h, s_send, 1, core).wait_send()

        @pl.when(g >= 2)
        def _():
            give(far, h, s_fwd, 0, core).wait_send()

    def drain(e, carry):
        cp, cj = carry
        p, j = digits(cp, cj)

        @pl.when(p == j)
        def _():
            panel_chunk(p).wait_send()

        for b in range(2):
            @pl.when(goes_up(p, b, j))
            def _():
                piece("wait_send", p, b, j, up_sem, up_id)

            @pl.when((z > 0) & (p >= z))
            def _():
                piece("wait_send", p, b, j, dn_sem, dn_id)

            @pl.when(goes_x(p, b, j) | ((p == z) & (b == x)))
            def _():
                piece("wait_send", p, b, j, xs_sem, x_id)

        return cp // nz, cj // nz

    lax.fori_loop(0, count, drain, (code_p, code_j))


def fused(nz):
    def run(f, bw, bp, pat, er, ep, pv):
        rows, order = f.shape[1:]
        pc, wc, total = bp.shape[2], bw.shape[2], ep.shape[1]
        dma = pltpu.SemaphoreType.DMA
        anywhere = pl.BlockSpec(memory_space=pl.ANY)
        return pl.pallas_call(
            functools.partial(panel_kernel, nz),
            out_shape=jax.ShapeDtypeStruct((pv.shape[0], wc), BF16),
            in_specs=[anywhere] * 3
            + [pl.BlockSpec(memory_space=pltpu.SMEM)]
            + [anywhere] * 3,
            out_specs=pl.BlockSpec(memory_space=pltpu.VMEM),
            scratch_shapes=[
                pltpu.VMEM((2 * nz, rows, order), BF16),
                pltpu.VMEM((order, wc), BF16),
                pltpu.VMEM((2, order, pc), BF16),
                pltpu.VMEM(er.shape, BF16),
                pltpu.VMEM(ep.shape, BF16),
                pltpu.VMEM(pv.shape, BF16),
                pltpu.VMEM((2 * pc + wc, order), BF16),
                pltpu.VMEM((2 * pc + wc, order), F32),
                pltpu.VMEM((4, total // 4, wc), F32),
                pltpu.VMEM((2, total // 4, wc), F32),
                pltpu.VMEM((total // 4, wc), BF16),
                pltpu.VMEM((total // 4, wc), BF16),
                pltpu.VMEM((4, total // 4, wc), BF16),
                dma((6,)),
                dma((2 * nz, nz + 1)),
                dma((2 * nz, nz + 1)),
                dma((2 * nz, nz + 1)),
                dma((2 * nz, nz + 1)),
                dma((nz,)),
                dma((nz,)),
                dma((3,)),
                dma((3,)),
                dma((2,)),
                dma((2,)),
                dma((2, 2)),
                dma((1, 2)),
                dma((4, 2)),
            ],
            compiler_params=pltpu.CompilerParams(
                collective_id=0, has_side_effects=True, vmem_limit_bytes=60 * 2**20
            ),
        )(f, bw, bp, pat, er, ep, pv)

    return run


def fits(mesh, f, bw, bp, pat, er, ep, pv):
    nz = mesh.shape["scen"]
    order = f.shape[2]
    return (
        mesh.shape["slab"] == 2
        and mesh.shape["grp"] == 4
        and nz >= 2
        and order % (128 * nz) == 0
        and f.shape[1] * 2 * nz == order
        and f.shape[1] % 16 == 0
        and bw.shape[2] % 256 == 0
        and bp.shape[2] % 256 == 0
        and ep.shape[1] == 2 * bp.shape[2]
        and ep.shape[1] % 512 == 0
        and pv.shape[0] * 4 == ep.shape[1]
        and (bw.shape[2] // pat.shape[1]) % 128 == 0
        and nz ** (nz * (nz + 1) // 2) < 2**31
    )


def body(
    factor_inverse,
    border_window,
    border_panel,
    border_pattern,
    earlier_rows,
    earlier_panel,
    pivot_inverse,
):
    window = border_window[0]
    columns = window.shape[1]
    blocks = border_pattern.shape[1]
    column_mask = jnp.repeat(border_pattern[0].astype(jnp.bfloat16), columns // blocks)
    masked = window * column_mask[None, :]
    panel_border = border_panel[0]
    incoming = lax.all_gather(factor_inverse[0], ("scen", "slab"), axis=0, tiled=True)
    window_sum = lax.dot_general(
        incoming, masked, (((0,), (0,)), ((), ())), preferred_element_type=jnp.float32
    )
    panel_sum = lax.dot_general(
        panel_border, incoming, (((0,), (0,)), ((), ())), preferred_element_type=jnp.float32
    )
    window_sum, panel_sum = (window_sum, panel_sum)
    window_image = window_sum.astype(jnp.bfloat16)
    panel_piece = panel_sum.astype(jnp.bfloat16)
    panel_image = lax.all_gather(panel_piece, "slab", axis=0, tiled=True)
    contribution = jnp.dot(panel_image, window_image, preferred_element_type=jnp.float32)
    update = lax.dot_general(
        earlier_panel, earlier_rows, (((0,), (0,)), ((), ())), preferred_element_type=jnp.float32
    )
    partial_sum = contribution - update
    schur_block = lax.psum(partial_sum, "grp").astype(jnp.bfloat16)
    return jnp.dot(pivot_inverse, schur_block, preferred_element_type=jnp.float32).astype(
        jnp.bfloat16
    )


def solution(mesh):
    placed = (
        P("grp", ("scen", "slab"), None),
        P("grp", None, ("scen", "slab")),
        P("grp", None, "slab"),
        P("grp", ("scen", "slab")),
        P("grp", ("scen", "slab")),
        P("grp", None),
        P("grp", None),
    )

    def either(*blocks):
        if fits(mesh, *blocks):
            return fused(mesh.shape["scen"])(*blocks)
        return body(*blocks)

    return jax.shard_map(
        either, mesh=mesh, in_specs=placed, out_specs=P("grp", ("scen", "slab")), check_vma=False
    )
```
